256 devices in a mesh: tab: 64 (over x, z, core), rep: 4 (over y).
Axes of the slice: x: 4, y: 4, z: 8, core: 2. Of those that a mesh axis runs over, the one named last changes fastest.
Arguments:
- sample_ids: int32 [131072, 26], P(('tab', 'rep')), may hold values from 0 to 32767, as said below
- features: bfloat16 [131072, 27, 128], P(('tab', 'rep')), may hold values from -6 to 6
- pair_grad: bfloat16 [351, 131072], P(None, ('tab', 'rep')), may hold values from -1.59375 to 1.59375
Outputs:
- table_grad: float32 [26, 32768, 128], P(None, ('tab', 'rep'))
- dense_grad: float32 [131072, 128], P(('tab', 'rep'))
The draws below stay inside these ranges and needn't reach their ends.
Inputs may be any that keep to these rules, and one draw needn't show every extreme that they name: `sample_ids`: row r is owned by device r // 128, numbered tab * 4 + rep. For each field and the 512 samples of one device (aligned blocks of rows in device order), at most 4 ids fall in the rows of any one device, and at most 16 in the rows of any one tab index; in every block and field both bounds are reached.
All inputs are finite; a program needn't handle non-finite values.
Results may differ from the reference program's by a relative error of at most 0.0029.
Values may be sent and summed in bfloat16 or wider, within the bound.
A program may use at most 128 MiB of HBM per device.

```python
import math
import jax
import jax.numpy as jnp
import numpy as np
from jax import lax

E = 128
F = 26
B_DEV = 512
RQ = 128
PAIRS = 351
BATCH = 131072
ROWS = 32768
CAP = 4
N_TAB = 64
N_REP = 4


def draw_sample_ids(key, part):
    blocks = N_TAB * N_REP
    key_hot = jax.random.fold_in(key, 11)
    key_pick = jax.random.fold_in(key, 12)
    key_mix = jax.random.fold_in(key, 13)
    key_rows = jax.random.fold_in(key, 14)
    hot_col = jax.random.randint(key_hot, (blocks * F, 1), 0, N_TAB)
    others = (blocks - N_REP) * CAP
    picks = jax.vmap(lambda k: jax.random.permutation(k, others))(jax.random.split(key_pick, blocks * F))
    chosen = picks[:, :B_DEV - N_REP * CAP] // CAP
    cold_owner = chosen + jnp.where(chosen >= hot_col * N_REP, N_REP, 0)
    hot_owner = hot_col * N_REP + (jnp.arange(N_REP * CAP, dtype=jnp.int32) // CAP)[None, :]
    all_owner = jnp.concatenate([hot_owner, cold_owner], axis=1)
    orders = jax.vmap(lambda k: jax.random.permutation(k, B_DEV))(jax.random.split(key_mix, blocks * F))
    all_owner = jnp.take_along_axis(all_owner, orders, axis=1)
    within = jax.random.randint(key_rows, all_owner.shape, 0, RQ)
    result = (all_owner * RQ + within).astype(jnp.int32)
    return result.reshape(blocks, F, B_DEV).transpose(0, 2, 1).reshape(blocks * B_DEV, F)


def steps_of(own_key, dims, pieces, smallest, top_value):
    def one(axis_at, parts):
        heights = jax.random.uniform(jax.random.fold_in(jax.random.fold_in(own_key, 6), axis_at), (parts,), jnp.float32, smallest / len(pieces), top_value / len(pieces))
        return jnp.repeat(jnp.exp(heights), dims[axis_at] // parts).reshape((-1,) + (1,) * (len(dims) - axis_at - 1))

    loudness = one(*pieces[0])
    for cut in pieces[1:]:
        loudness = loudness * one(*cut)
    return loudness


def noise(own_key, shape, width, limit, shards=(), held_as=jnp.bfloat16):
    level = steps_of(own_key, shape, shards, -0.22, 0.18) if shards else 1.0
    entries = jax.random.normal(own_key, shape, jnp.float32) * width * level
    return jnp.minimum(jnp.maximum(entries, -limit), limit).astype(held_as)


def setup_inputs(seed: int = 0) -> dict:
    key_list = jax.random.split(jax.random.key(seed), 4)
    sample_ids = draw_sample_ids(jax.random.fold_in(key_list[3], 71), 0)
    features = noise(key_list[1], (BATCH, F + 1, E), 1.0, 6.0, ((0, 256),))
    pair_grad = noise(key_list[2], (PAIRS, BATCH), 0.2, 1.59375, ((1, 256),))
    return {"sample_ids": sample_ids, "features": features, "pair_grad": pair_grad}


def pair_table(vectors):
    row_of, col_of = np.tril_indices(vectors, -1)
    spread = np.zeros((row_of.shape[0], vectors * vectors), np.float32)
    places = np.arange(row_of.shape[0])
    spread[places, row_of * vectors + col_of] = 1.0
    spread[places, col_of * vectors + row_of] = 1.0
    return spread


def reference(sample_ids, features, pair_grad):
    vectors = features.shape[1]
    spread = jnp.asarray(pair_table(vectors).T).astype(jnp.bfloat16)
    symmetric = jnp.dot(spread, pair_grad, preferred_element_type=jnp.float32)
    block_rows = math.gcd(BATCH, 4096)
    block_count = BATCH // block_rows

    def one_block(running, index):
        start = (index * block_rows).astype(jnp.int32)
        part_feat = lax.dynamic_slice_in_dim(features, start, block_rows, 0).astype(jnp.float32)
        part_sym = lax.dynamic_slice_in_dim(symmetric, start, block_rows, 1).reshape(vectors, vectors, block_rows)
        part_ids = lax.dynamic_slice_in_dim(sample_ids, start, block_rows, 0)
        gradients = jnp.einsum("fgb,bge->bfe", part_sym, part_feat)
        rounded = lax.optimization_barrier(gradients[:, 1:, :].astype(jnp.bfloat16)).astype(jnp.float32)
        fields_at = jnp.broadcast_to(jnp.arange(F, dtype=jnp.int32)[None, :], part_ids.shape)
        running = running.at[fields_at, part_ids].add(rounded)
        return running, gradients[:, 0, :]

    start_grad = jnp.zeros((F, ROWS, E), jnp.float32)
    table_grad, dense_parts = lax.scan(one_block, start_grad, jnp.arange(block_count, dtype=jnp.int32))
    return table_grad, dense_parts.reshape(BATCH, E)
```

```python
import functools

import jax
import jax.numpy as jnp
import numpy as np
from jax import lax
from jax.experimental import pallas as pl
from jax.experimental.pallas import tpu as pltpu
from jax.sharding import PartitionSpec as P

RQ = 128
CAP = 4
B = 512
F = 26
E = 128
NZ = 8
NG = 32
GS = NZ * CAP
SLOTS = NG * GS
FC = 2
C = F // FC
AHEAD = 4
QUADS = 7
MESH = pl.DeviceIdType.MESH
BF = jnp.bfloat16
F32 = jnp.float32


def pair_table(vectors):
    row_of, col_of = np.tril_indices(vectors, -1)
    spread = np.zeros((row_of.shape[0], vectors * vectors), np.float32)
    places = np.arange(row_of.shape[0])
    spread[places, row_of * vectors + col_of] = 1.0
    spread[places, col_of * vectors + row_of] = 1.0
    return spread


def device_of(group, z):
    x, core, y = group // 8, (group // 4) % 2, group % 4
    return ((x * NZ + z) * 2 + core, y)


def iota(shape, dim):
    return lax.broadcasted_iota(jnp.int32, shape, dim)


def exchange_kernel(
    ids_ref, ids_t_ref, grads_hbm, out_ref,
    grads, slot_rows, slot_cols, tag_send, tag_recv, wanted, send, recv, part, rows_f32, ring,
    load_sem, send_sem, recv_sem, tag_send_sem, tag_recv_sem, ring_send_sem, ring_recv_sem,
):
    tab = lax.axis_index("tab")
    y = lax.axis_index("rep")
    x, z, core = tab // (NZ * 2), (tab // 2) % NZ, tab % 2
    me = (x * 2 + core) * 4 + y

    barrier = pltpu.get_barrier_semaphore()
    up = device_of(me, lax.rem(z + 1, NZ))
    down = device_of(me, lax.rem(z + NZ - 1, NZ))

    @pl.loop(1, NG)
    def _(i):
        pl.semaphore_signal(barrier, inc=1, device_id=device_of(lax.rem(me + i, NG), z), device_id_type=MESH)

    pl.semaphore_signal(barrier, inc=1, device_id=up, device_id_type=MESH)
    pl.semaphore_signal(barrier, inc=1, device_id=down, device_id_type=MESH)

    load = pltpu.make_async_copy(grads_hbm, grads, load_sem)
    load.start()

    slot_rows[...] = jnp.zeros(slot_rows.shape, F32)

    @pl.loop(0, QUADS)
    def _(quad):
        shifted = pltpu.roll(ids_ref[...], lax.rem(128 - 4 * quad, 128), 1)
        for q in range(4):
            field = quad * 4 + q
            own_c = shifted[:, q : q + 1] >> 7
            own_r = ids_t_ref[pl.ds(field, 1), :] >> 7
            pieces = []
            for block in range(B // 128):
                lanes = own_r[:, block * 128 : (block + 1) * 128]
                total = jnp.zeros((1, 128), F32)
                for other in range(block + 1):
                    same = own_c[other * 128 : (other + 1) * 128] == lanes
                    if other == block:
                        same = same & (iota((128, 128), 0) < iota((128, 128), 1))
                    total = total + jnp.sum(jnp.where(same, 1.0, 0.0), axis=0, keepdims=True)
                pieces.append(total)
            rank = jnp.concatenate(pieces, axis=1).astype(jnp.int32)
            group = ((own_r >> 6) << 3) | (own_r & 7)
            slot = group * GS + ((own_r >> 3) & 7) * CAP + rank
            slot_rows[pl.ds(field, 1), :] = slot.astype(F32)

    slot_cols[...] = slot_rows[...].T.astype(jnp.int32)

    @pl.loop(0, QUADS)
    def _(quad):
        back = lax.rem(128 - 4 * quad, 128)
        ids = pltpu.roll(ids_ref[...], back, 1)
        slots = pltpu.roll(slot_cols[...], back, 1)
        total = jnp.zeros((NG, 128), F32)
        for q in range(4):
            tag = ((ids[:, q : q + 1] & (RQ - 1)) + 1).astype(F32)
            place = (slots[:, q : q + 1] & (GS - 1)) + q * GS
            right = jnp.where(iota((B, 128), 1) == place, tag, 0.0).astype(BF)
            row = slot_rows[pl.ds(quad * 4 + q, 1), :].astype(jnp.int32)
            left = jnp.where(iota((NG, B), 0) == (row >> 5), 1.0, 0.0).astype(BF)
            total = total + jnp.dot(left, right, preferred_element_type=F32)
        tag_send[pl.ds(quad, NG, stride=8), :] = total

    tag_send[pl.ds(QUADS, NG, stride=8), :] = jnp.zeros((NG, 128), F32)
    pl.semaphore_wait(barrier, NG + 1)

    def rows8(g):
        return pl.ds(pl.multiple_of(g * 8, 8), 8)

    @pl.loop(1, NG)
    def _(i):
        g = lax.rem(me + i, NG)
        pltpu.make_async_remote_copy(
            src_ref=tag_send.at[rows8(g)], dst_ref=tag_recv.at[rows8(me)],
            send_sem=tag_send_sem, recv_sem=tag_recv_sem, device_id=device_of(g, z), device_id_type=MESH,
        ).start()

    pltpu.make_async_copy(tag_send.at[rows8(me)], tag_recv.at[rows8(me)], tag_recv_sem).start()
    load.wait()

    def place(chunk):
        @pl.loop(0, FC)
        def _(k):
            field = chunk * FC + k
            row = slot_rows[pl.ds(field, 1), :].astype(jnp.int32)
            data = grads[field]
            half = SLOTS // 2
            for h in range(2):
                hit = iota((half, B), 0) + h * half == row
                placed = jnp.dot(jnp.where(hit, 1.0, 0.0).astype(BF), data, preferred_element_type=F32)
                send[chunk, pl.ds(h * NG // 2, NG // 2), pl.ds(pl.multiple_of(k * GS, GS), GS), :] = (
                    placed.astype(BF).reshape(NG // 2, GS, E)
                )

        pltpu.make_async_copy(send.at[chunk, me], recv.at[chunk, me], recv_sem.at[chunk]).start()

        @pl.loop(1, NG)
        def _(i):
            g = lax.rem(me + i, NG)
            pltpu.make_async_remote_copy(
                src_ref=send.at[chunk, g], dst_ref=recv.at[chunk, me],
                send_sem=send_sem, recv_sem=recv_sem.at[chunk], device_id=device_of(g, z), device_id_type=MESH,
            ).start()

    @pl.loop(0, AHEAD)
    def _(chunk):
        place(chunk)

    pltpu.make_async_copy(tag_recv, tag_recv, tag_recv_sem).wait()
    tags = tag_recv[...].astype(BF)
    for q in range(4):
        col = iota((128, SLOTS), 1)
        spread = jnp.where(iota((128, SLOTS), 0) == q * GS + (col >> 9) * 16 + (col & 15), 1.0, 0.0).astype(BF)
        wide = jnp.dot(tags, spread, preferred_element_type=F32).reshape(NG, 8, SLOTS)
        source = (iota((NG, 8, SLOTS), 2) & 511) >> 4
        tag = jnp.sum(jnp.where(iota((NG, 8, SLOTS), 0) == source, wide, 0.0), axis=0).astype(jnp.int32)
        row = ((iota((8, SLOTS), 1) & 15) >> 2) * RQ + tag - 1
        wanted[q] = jnp.where(tag > 0, row, -1)

    def tally(chunk):
        pltpu.make_async_copy(recv.at[chunk], recv.at[chunk], recv_sem.at[chunk]).wait()

        @pl.loop(0, FC)
        def _(k):
            field = chunk * FC + k
            want = wanted[field % 4, pl.ds(field // 4, 1), :]
            for h in range(2):
                data = recv[chunk, :, pl.ds(pl.multiple_of(k * GS + h * 16, 16), 16), :].reshape(NG * 16, E)
                hit = iota((4 * RQ, NG * 16), 0) == want[:, h * 512 : (h + 1) * 512]
                rows = jnp.dot(jnp.where(hit, 1.0, 0.0).astype(BF), data, preferred_element_type=F32)
                rows_f32[pl.ds(h * 4 * RQ, 4 * RQ), :] = rows
                part[chunk, pl.ds(h * 4, 4), pl.ds(pl.multiple_of(k * RQ, RQ), RQ), :] = rows.astype(BF).reshape(4, RQ, E)
            out_ref[field] = rows_f32[pl.ds(pl.multiple_of(z * RQ, RQ), RQ), :]

    def owner(d, step):
        away = 4 - step
        return lax.rem(z + (away if d == 0 else NZ - away), NZ)

    def arrived(d, step, chunk):
        size = FC * RQ if step else RQ
        ref = ring.at[d, step, chunk, pl.ds(0, size)]
        pltpu.make_async_copy(ref, ref, ring_recv_sem.at[d, step, chunk]).wait()

    def add(step, chunk):
        for d in range(2):
            arrived(d, step - 1, chunk)
            o = owner(d, step)
            if step == 1:
                part[chunk, o, pl.ds(d * RQ, RQ), :] = (
                    part[chunk, o, pl.ds(d * RQ, RQ), :].astype(F32) + ring[d, 0, chunk, pl.ds(0, RQ), :].astype(F32)
                ).astype(BF)
            else:
                part[chunk, o] = (part[chunk, o].astype(F32) + ring[d, step - 1, chunk].astype(F32)).astype(BF)

    def forward(step, chunk):
        for d in range(2):
            o = owner(d, step)
            src = part.at[chunk, o, pl.ds(d * RQ, RQ)] if step == 0 else part.at[chunk, o]
            dst = ring.at[d, 0, chunk, pl.ds(0, RQ)] if step == 0 else ring.at[d, step, chunk]
            pltpu.make_async_remote_copy(
                src_ref=src, dst_ref=dst, send_sem=ring_send_sem.at[d], recv_sem=ring_recv_sem.at[d, step, chunk],
                device_id=up if d == 0 else down, device_id_type=MESH,
            ).start()

    def finish(chunk):
        for d in range(2):
            arrived(d, 3, chunk)
        both = ring[0, 3, chunk].astype(F32) + ring[1, 3, chunk].astype(F32)
        for k in range(FC):
            out_ref[chunk * FC + k] += both[k * RQ : (k + 1) * RQ]

    @pl.loop(0, C + 4)
    def _(t):
        @pl.when(t + AHEAD < C)
        def _():
            place(t + AHEAD)

        @pl.when(t < C)
        def _():
            tally(t)

        for step in range(1, 4):

            @pl.when((t >= step) & (t < C + step))
            def _():
                add(step, t - step)

        @pl.when(t >= 4)
        def _():
            finish(t - 4)

        for step in range(4):

            @pl.when((t >= step) & (t < C + step))
            def _():
                forward(step, t - step)

    sent = send.at[:, pl.ds(0, NG - 1)]
    pltpu.make_async_copy(sent, sent, send_sem).wait()
    tags_sent = tag_send.at[pl.ds(0, (NG - 1) * 8)]
    pltpu.make_async_copy(tags_sent, tags_sent, tag_send_sem).wait()
    for d in range(2):
        for step in range(4):
            ref = ring.at[d, step, :, pl.ds(0, FC * RQ if step else RQ)]
            pltpu.make_async_copy(ref, ref, ring_send_sem.at[d]).wait()


def exchange(ids, ids_t, grads):
    vmem = pl.BlockSpec(memory_space=pltpu.VMEM)
    dma = pltpu.SemaphoreType.DMA
    return pl.pallas_call(
        exchange_kernel,
        out_shape=jax.ShapeDtypeStruct((F, RQ, E), F32),
        in_specs=[vmem, vmem, pl.BlockSpec(memory_space=pl.ANY)],
        out_specs=vmem,
        scratch_shapes=[
            pltpu.VMEM((F, B, E), BF),
            pltpu.VMEM((128, B), F32),
            pltpu.VMEM((B, 128), jnp.int32),
            pltpu.VMEM((NG * 8, 128), F32),
            pltpu.VMEM((NG * 8, 128), F32),
            pltpu.VMEM((4, 8, SLOTS), jnp.int32),
            pltpu.VMEM((C, NG, FC * GS, E), BF),
            pltpu.VMEM((C, NG, FC * GS, E), BF),
            pltpu.VMEM((C, NZ, FC * RQ, E), BF),
            pltpu.VMEM((NZ * RQ, E), F32),
            pltpu.VMEM((2, 4, C, FC * RQ, E), BF),
            dma, dma, dma((C,)), dma, dma, dma((2,)), dma((2, 4, C)),
        ],
        compiler_params=pltpu.CompilerParams(
            collective_id=0, has_side_effects=True, vmem_limit_bytes=60 * 2**20
        ),
        name="exchange",
    )(ids, ids_t, grads)


def local(sample_ids, features, pair_grad):
    vectors = features.shape[1]
    samples = features.shape[0]
    spread = jnp.asarray(pair_table(vectors).T).astype(BF)
    symmetric = jnp.dot(spread, pair_grad, preferred_element_type=F32)
    symmetric = symmetric.astype(BF).reshape(vectors, vectors, samples)
    gradients = jnp.einsum("fgb,bge->fbe", symmetric, features, preferred_element_type=F32)
    dense_grad = gradients[0]
    field_grads = gradients[1:].astype(BF)
    ids = jnp.pad(sample_ids, ((0, 0), (0, 128 - F)))
    ids_t = jnp.pad(sample_ids.T, ((0, 32 - F), (0, 0)))
    return (exchange(ids, ids_t, field_grads), dense_grad)


def solution(mesh):
    placed = (P(("tab", "rep"), None), P(("tab", "rep"), None, None), P(None, ("tab", "rep")))
    return jax.shard_map(
        local,
        mesh=mesh,
        in_specs=placed,
        out_specs=(P(None, ("tab", "rep"), None), P(("tab", "rep"), None)),
        check_vma=False,
    )
```

```python
import functools

import jax
import jax.numpy as jnp
import numpy as np
from jax import lax
from jax.experimental import pallas as pl
from jax.experimental.pallas import tpu as pltpu
from jax.sharding import PartitionSpec as P

RQ = 128
CAP = 4
B = 512
F = 26
E = 128
NZ = 8
NG = 32
GS = NZ * CAP
SLOTS = NG * GS
FC = 2
C = F // FC
AHEAD = 4
QUADS = 7
MESH = pl.DeviceIdType.MESH
BF = jnp.bfloat16
F32 = jnp.float32


V = F + 1
PAIRS = V * F // 2
SB = 16
NB = B // SB


def pair_table():
    row_of, col_of = np.tril_indices(V, -1)
    spread = np.zeros((384, QUADS * 128), np.float32)
    places = np.arange(PAIRS)
    spread[places, row_of * 32 + col_of] = 1.0
    spread[places, col_of * 32 + row_of] = 1.0
    return spread


def device_of(group, z):
    x, core, y = group // 8, (group // 4) % 2, group % 4
    return ((x * NZ + z) * 2 + core, y)


def iota(shape, dim):
    return lax.broadcasted_iota(jnp.int32, shape, dim)


def exchange_kernel(
    ids_ref, feats_hbm, pairs_ref, table_ref, out_ref, dense_ref,
    feats, pairs, picked, expand, left, grads, ids_rows, ids_cols, slot_rows, slot_cols, tag_send, tag_recv, wanted, send, recv, part, rows_f32, ring,
    load_sem, send_sem, recv_sem, tag_send_sem, tag_recv_sem, ring_send_sem, ring_recv_sem,
):
    tab = lax.axis_index("tab")
    y = lax.axis_index("rep")
    x, z, core = tab // (NZ * 2), (tab // 2) % NZ, tab % 2
    me = (x * 2 + core) * 4 + y

    barrier = pltpu.get_barrier_semaphore()
    up = device_of(me, lax.rem(z + 1, NZ))
    down = device_of(me, lax.rem(z + NZ - 1, NZ))

    @pl.loop(1, NG)
    def _(i):
        pl.semaphore_signal(barrier, inc=1, device_id=device_of(lax.rem(me + i, NG), z), device_id_type=MESH)

    pl.semaphore_signal(barrier, inc=1, device_id=up, device_id_type=MESH)
    pl.semaphore_signal(barrier, inc=1, device_id=down, device_id_type=MESH)

    load = pltpu.make_async_copy(feats_hbm, feats, load_sem)
    load.start()

    pairs[...] = jnp.zeros(pairs.shape, F32)
    pairs[pl.ds(0, PAIRS), :] = pairs_ref[...].astype(F32)
    by_sample = pairs[...].T.astype(BF)
    for quad in range(QUADS):
        picked[quad] = jnp.dot(
            by_sample, table_ref[:, quad * 128 : (quad + 1) * 128], preferred_element_type=F32
        ).astype(BF)
    for q in range(4):
        expand[q] = jnp.where(
            iota((128, 32 * SB), 0) == q * 32 + (iota((128, 32 * SB), 1) >> 4), 1.0, 0.0
        ).astype(BF)

    @pl.loop(0, QUADS)
    def _(quad):
        @pl.loop(0, 4)
        def _(q):
            wide = jnp.dot(picked[quad], expand[q], preferred_element_type=F32).reshape(NB, SB, 32 * SB)
            own = iota((1, SB, 32 * SB), 1) == (iota((1, SB, 32 * SB), 2) & (SB - 1))
            left[:, pl.ds(pl.multiple_of((quad * 4 + q) * SB, SB), SB), :] = jnp.where(own, wide, 0.0).astype(BF)

    load.wait()

    @pl.loop(0, NB)
    def _(g):
        at = pl.ds(pl.multiple_of(g * SB, SB), SB)
        right = jnp.concatenate([feats[:, at, :], jnp.zeros((32 - V, SB, E), BF)], axis=0).reshape(32 * SB, E)
        result = jnp.dot(left[g], right, preferred_element_type=F32).reshape(4 * QUADS, SB, E)
        dense_ref[at, :] = result[0]
        grads[:, at, :] = result[1:V].astype(BF)

    ids_rows[...] = jnp.zeros(ids_rows.shape, F32)
    ids_rows[pl.ds(0, F), :] = ids_ref[...].astype(F32)
    ids_cols[...] = ids_rows[...].T.astype(jnp.int32)

    slot_rows[...] = jnp.zeros(slot_rows.shape, F32)

    def rank_quad(quad):
        shifted = pltpu.roll(ids_cols[...], lax.rem(128 - 4 * quad, 128), 1)
        for q in range(4):
            field = quad * 4 + q
            own_c = shifted[:, q : q + 1] >> 7
            own_r = ids_rows[pl.ds(field, 1), :].astype(jnp.int32) >> 7
            pieces = []
            for block in range(B // 128):
                lanes = own_r[:, block * 128 : (block + 1) * 128]
                total = jnp.zeros((1, 128), F32)
                for other in range(block + 1):
                    same = own_c[other * 128 : (other + 1) * 128] == lanes
                    if other == block:
                        same = same & (iota((128, 128), 0) < iota((128, 128), 1))
                    total = total + jnp.sum(jnp.where(same, 1.0, 0.0), axis=0, keepdims=True)
                pieces.append(total)
            rank = jnp.concatenate(pieces, axis=1).astype(jnp.int32)
            group = ((own_r >> 6) << 3) | (own_r & 7)
            slot = group * GS + ((own_r >> 3) & 7) * CAP + rank
            slot_rows[pl.ds(field, 1), :] = slot.astype(F32)

    def place(chunk):
        @pl.loop(0, FC)
        def _(k):
            field = chunk * FC + k
            row = slot_rows[pl.ds(field, 1), :].astype(jnp.int32)
            data = grads[field]
            half = SLOTS // 2
            for h in range(2):
                hit = iota((half, B), 0) + h * half == row
                placed = jnp.dot(jnp.where(hit, 1.0, 0.0).astype(BF), data, preferred_element_type=F32)
                send[chunk, pl.ds(h * NG // 2, NG // 2), pl.ds(pl.multiple_of(k * GS, GS), GS), :] = (
                    placed.astype(BF).reshape(NG // 2, GS, E)
                )

        pltpu.make_async_copy(send.at[chunk, me], recv.at[chunk, me], recv_sem.at[chunk]).start()

        @pl.loop(1, NG)
        def _(i):
            g = lax.rem(me + i, NG)
            pltpu.make_async_remote_copy(
                src_ref=send.at[chunk, g], dst_ref=recv.at[chunk, me],
                send_sem=send_sem, recv_sem=recv_sem.at[chunk], device_id=device_of(g, z), device_id_type=MESH,
            ).start()

    pl.semaphore_wait(barrier, NG + 1)

    @pl.loop(0, AHEAD * FC // 4)
    def _(quad):
        rank_quad(quad)

        @pl.loop(0, 4 // FC)
        def _(i):
            place(quad * (4 // FC) + i)

    @pl.loop(AHEAD * FC // 4, QUADS)
    def _(quad):
        rank_quad(quad)

    slot_cols[...] = slot_rows[...].T.astype(jnp.int32)

    @pl.loop(0, QUADS)
    def _(quad):
        back = lax.rem(128 - 4 * quad, 128)
        ids = pltpu.roll(ids_cols[...], back, 1)
        slots = pltpu.roll(slot_cols[...], back, 1)
        total = jnp.zeros((NG, 128), F32)
        for q in range(4):
            tag = ((ids[:, q : q + 1] & (RQ - 1)) + 1).astype(F32)
            place = (slots[:, q : q + 1] & (GS - 1)) + q * GS
            right = jnp.where(iota((B, 128), 1) == place, tag, 0.0).astype(BF)
            row = slot_rows[pl.ds(quad * 4 + q, 1), :].astype(jnp.int32)
            group = jnp.where(iota((NG, B), 0) == (row >> 5), 1.0, 0.0).astype(BF)
            total = total + jnp.dot(group, right, preferred_element_type=F32)
        tag_send[pl.ds(quad, NG, stride=8), :] = total

    tag_send[pl.ds(QUADS, NG, stride=8), :] = jnp.zeros((NG, 128), F32)
    def rows8(g):
        return pl.ds(pl.multiple_of(g * 8, 8), 8)

    @pl.loop(1, NG)
    def _(i):
        g = lax.rem(me + i, NG)
        pltpu.make_async_remote_copy(
            src_ref=tag_send.at[rows8(g)], dst_ref=tag_recv.at[rows8(me)],
            send_sem=tag_send_sem, recv_sem=tag_recv_sem, device_id=device_of(g, z), device_id_type=MESH,
        ).start()

    pltpu.make_async_copy(tag_send.at[rows8(me)], tag_recv.at[rows8(me)], tag_recv_sem).start()
    pltpu.make_async_copy(tag_recv, tag_recv, tag_recv_sem).wait()
    tags = tag_recv[...].astype(BF)
    for q in range(4):
        col = iota((128, SLOTS), 1)
        spread = jnp.where(iota((128, SLOTS), 0) == q * GS + (col >> 9) * 16 + (col & 15), 1.0, 0.0).astype(BF)
        wide = jnp.dot(tags, spread, preferred_element_type=F32).reshape(NG, 8, SLOTS)
        source = (iota((NG, 8, SLOTS), 2) & 511) >> 4
        tag = jnp.sum(jnp.where(iota((NG, 8, SLOTS), 0) == source, wide, 0.0), axis=0).astype(jnp.int32)
        row = ((iota((8, SLOTS), 1) & 15) >> 2) * RQ + tag - 1
        wanted[q] = jnp.where(tag > 0, row, -1)

    def tally(chunk):
        pltpu.make_async_copy(recv.at[chunk], recv.at[chunk], recv_sem.at[chunk]).wait()

        @pl.loop(0, FC)
        def _(k):
            field = chunk * FC + k
            want = wanted[field % 4, pl.ds(field // 4, 1), :]
            for h in range(2):
                data = recv[chunk, :, pl.ds(pl.multiple_of(k * GS + h * 16, 16), 16), :].reshape(NG * 16, E)
                hit = iota((4 * RQ, NG * 16), 0) == want[:, h * 512 : (h + 1) * 512]
                rows = jnp.dot(jnp.where(hit, 1.0, 0.0).astype(BF), data, preferred_element_type=F32)
                rows_f32[pl.ds(h * 4 * RQ, 4 * RQ), :] = rows
                part[chunk, pl.ds(h * 4, 4), pl.ds(pl.multiple_of(k * RQ, RQ), RQ), :] = rows.astype(BF).reshape(4, RQ, E)
            out_ref[field] = rows_f32[pl.ds(pl.multiple_of(z * RQ, RQ), RQ), :]

    def owner(d, step):
        away = 4 - step
        return lax.rem(z + (away if d == 0 else NZ - away), NZ)

    def arrived(d, step, chunk):
        size = FC * RQ if step else RQ
        ref = ring.at[d, step, chunk, pl.ds(0, size)]
        pltpu.make_async_copy(ref, ref, ring_recv_sem.at[d, step, chunk]).wait()

    def add(step, chunk):
        for d in range(2):
            arrived(d, step - 1, chunk)
            o = owner(d, step)
            if step == 1:
                part[chunk, o, pl.ds(d * RQ, RQ), :] = (
                    part[chunk, o, pl.ds(d * RQ, RQ), :].astype(F32) + ring[d, 0, chunk, pl.ds(0, RQ), :].astype(F32)
                ).astype(BF)
            else:
                part[chunk, o] = (part[chunk, o].astype(F32) + ring[d, step - 1, chunk].astype(F32)).astype(BF)

    def forward(step, chunk):
        for d in range(2):
            o = owner(d, step)
            src = part.at[chunk, o, pl.ds(d * RQ, RQ)] if step == 0 else part.at[chunk, o]
            dst = ring.at[d, 0, chunk, pl.ds(0, RQ)] if step == 0 else ring.at[d, step, chunk]
            pltpu.make_async_remote_copy(
                src_ref=src, dst_ref=dst, send_sem=ring_send_sem.at[d], recv_sem=ring_recv_sem.at[d, step, chunk],
                device_id=up if d == 0 else down, device_id_type=MESH,
            ).start()

    def finish(chunk):
        for d in range(2):
            arrived(d, 3, chunk)
        both = ring[0, 3, chunk].astype(F32) + ring[1, 3, chunk].astype(F32)
        for k in range(FC):
            out_ref[chunk * FC + k] += both[k * RQ : (k + 1) * RQ]

    lag = (0, 2, 3, 4, 5)

    @pl.loop(0, C + lag[4])
    def _(t):
        for step in range(1, 4):

            @pl.when((t >= lag[step]) & (t < C + lag[step]))
            def _():
                add(step, t - lag[step])

        for step in range(1, 4):

            @pl.when((t >= lag[step]) & (t < C + lag[step]))
            def _():
                forward(step, t - lag[step])

        @pl.when(t + AHEAD < C)
        def _():
            place(t + AHEAD)

        @pl.when(t < C)
        def _():
            tally(t)
            forward(0, t)

        @pl.when(t >= lag[4])
        def _():
            finish(t - lag[4])

    sent = send.at[:, pl.ds(0, NG - 1)]
    pltpu.make_async_copy(sent, sent, send_sem).wait()
    tags_sent = tag_send.at[pl.ds(0, (NG - 1) * 8)]
    pltpu.make_async_copy(tags_sent, tags_sent, tag_send_sem).wait()
    for d in range(2):
        for step in range(4):
            ref = ring.at[d, step, :, pl.ds(0, FC * RQ if step else RQ)]
            pltpu.make_async_copy(ref, ref, ring_send_sem.at[d]).wait()


def interact(ids_t, features, pair_grad, table):
    vmem = pl.BlockSpec(memory_space=pltpu.VMEM)
    dma = pltpu.SemaphoreType.DMA
    return pl.pallas_call(
        exchange_kernel,
        out_shape=(jax.ShapeDtypeStruct((F, RQ, E), F32), jax.ShapeDtypeStruct((B, E), F32)),
        in_specs=[vmem, pl.BlockSpec(memory_space=pl.ANY), vmem, vmem],
        out_specs=(vmem, vmem),
        scratch_shapes=[
            pltpu.VMEM((V, B, E), BF),
            pltpu.VMEM((384, B), F32),
            pltpu.VMEM((QUADS, B, 128), BF),
            pltpu.VMEM((4, 128, 32 * SB), BF),
            pltpu.VMEM((NB, 4 * QUADS * SB, 32 * SB), BF),
            pltpu.VMEM((F, B, E), BF),
            pltpu.VMEM((128, B), F32),
            pltpu.VMEM((B, 128), jnp.int32),
            pltpu.VMEM((128, B), F32),
            pltpu.VMEM((B, 128), jnp.int32),
            pltpu.VMEM((NG * 8, 128), F32),
            pltpu.VMEM((NG * 8, 128), F32),
            pltpu.VMEM((4, 8, SLOTS), jnp.int32),
            pltpu.VMEM((C, NG, FC * GS, E), BF),
            pltpu.VMEM((C, NG, FC * GS, E), BF),
            pltpu.VMEM((C, NZ, FC * RQ, E), BF),
            pltpu.VMEM((NZ * RQ, E), F32),
            pltpu.VMEM((2, 4, C, FC * RQ, E), BF),
            dma, dma, dma((C,)), dma, dma, dma((2,)), dma((2, 4, C)),
        ],
        compiler_params=pltpu.CompilerParams(
            collective_id=0, has_side_effects=True, vmem_limit_bytes=63 * 2**20
        ),
        name="interact",
    )(ids_t, features, pair_grad, table)


def local(sample_ids, features, pair_grad):
    table = jnp.asarray(pair_table()).astype(BF)
    return interact(sample_ids.T, features.transpose(1, 0, 2), pair_grad, table)


def solution(mesh):
    placed = (P(("tab", "rep"), None), P(("tab", "rep"), None, None), P(None, ("tab", "rep")))
    return jax.shard_map(
        local,
        mesh=mesh,
        in_specs=placed,
        out_specs=(P(None, ("tab", "rep"), None), P(("tab", "rep"), None)),
        check_vma=False,
    )
```

```python
import functools

import jax
import jax.numpy as jnp
import numpy as np
from jax import lax
from jax.experimental import pallas as pl
from jax.experimental.pallas import tpu as pltpu
from jax.sharding import PartitionSpec as P

RQ = 128
CAP = 4
B = 512
F = 26
E = 128
NZ = 8
NG = 32
GS = NZ * CAP
SLOTS = NG * GS
FC = 2
C = F // FC
AHEAD = 4
QUADS = 7
MESH = pl.DeviceIdType.MESH
BF = jnp.bfloat16
F32 = jnp.float32


V = F + 1
PAIRS = V * F // 2
SB = 8
NB = B // SB


def pair_table():
    row_of, col_of = np.tril_indices(V, -1)
    spread = np.zeros((384, QUADS * 128), np.float32)
    places = np.arange(PAIRS)
    spread[places, row_of * 32 + col_of] = 1.0
    spread[places, col_of * 32 + row_of] = 1.0
    return spread


def device_of(group, z):
    x, core, y = group // 8, (group // 4) % 2, group % 4
    return ((x * NZ + z) * 2 + core, y)


def iota(shape, dim):
    return lax.broadcasted_iota(jnp.int32, shape, dim)


def exchange_kernel(
    ids_ref, feats_hbm, pairs_ref, table_ref, out_ref, dense_ref,
    feats, pairs, picked, expand, left, grads, ids_rows, ids_cols, slot_rows, slot_cols, tag_send, tag_recv, wanted, send, recv, part, rows_f32, ring,
    load_sem, send_sem, recv_sem, tag_send_sem, tag_recv_sem, ring_send_sem, ring_recv_sem,
):
    tab = lax.axis_index("tab")
    y = lax.axis_index("rep")
    x, z, core = tab // (NZ * 2), (tab // 2) % NZ, tab % 2
    me = (x * 2 + core) * 4 + y

    barrier = pltpu.get_barrier_semaphore()
    up = device_of(me, lax.rem(z + 1, NZ))
    down = device_of(me, lax.rem(z + NZ - 1, NZ))

    @pl.loop(1, NG)
    def _(i):
        pl.semaphore_signal(barrier, inc=1, device_id=device_of(lax.rem(me + i, NG), z), device_id_type=MESH)

    pl.semaphore_signal(barrier, inc=1, device_id=up, device_id_type=MESH)
    pl.semaphore_signal(barrier, inc=1, device_id=down, device_id_type=MESH)

    load = pltpu.make_async_copy(feats_hbm, feats, load_sem)
    load.start()

    pairs[...] = jnp.zeros(pairs.shape, F32)
    pairs[pl.ds(0, PAIRS), :] = pairs_ref[...].astype(F32)
    by_sample = pairs[...].T.astype(BF)
    for quad in range(QUADS):
        picked[quad] = jnp.dot(
            by_sample, table_ref[:, quad * 128 : (quad + 1) * 128], preferred_element_type=F32
        ).astype(BF)
    for q in range(4):
        expand[q] = jnp.where(
            iota((128, 32 * SB), 0) == q * 32 + (iota((128, 32 * SB), 1) >> 3), 1.0, 0.0
        ).astype(BF)

    @pl.loop(0, QUADS)
    def _(quad):
        own = iota((1, SB, 32 * SB), 1) == (iota((1, SB, 32 * SB), 2) & (SB - 1))
        for pair in range(2):
            both = [
                jnp.dot(picked[quad], expand[pair * 2 + q], preferred_element_type=F32).reshape(NB, SB, 32 * SB)
                for q in range(2)
            ]
            both = jnp.concatenate([jnp.where(own, wide, 0.0) for wide in both], axis=1)
            left[:, pl.ds(pl.multiple_of((quad * 2 + pair) * 2 * SB, 2 * SB), 2 * SB), :] = both.astype(BF)

    load.wait()

    @pl.loop(0, NB // 2, unroll=4)
    def _(g):
        at = pl.ds(pl.multiple_of(g * 2 * SB, 2 * SB), 2 * SB)
        wide = feats[:, at, :].astype(F32)
        results = []
        for h in range(2):
            right = jnp.concatenate([wide[:, h * SB : (h + 1) * SB], jnp.zeros((32 - V, SB, E), F32)], axis=0)
            right = right.reshape(32 * SB, E).astype(BF)
            result = jnp.dot(left[g * 2 + h], right, preferred_element_type=F32)
            results.append(result.reshape(4 * QUADS, SB, E))
        result = jnp.concatenate(results, axis=1)
        dense_ref[at, :] = result[0]
        grads[:, at, :] = result[1:V].astype(BF)

    ids_rows[...] = jnp.zeros(ids_rows.shape, F32)
    ids_rows[pl.ds(0, F), :] = ids_ref[...].astype(F32)
    ids_cols[...] = ids_rows[...].T.astype(jnp.int32)

    slot_rows[...] = jnp.zeros(slot_rows.shape, F32)

    def rank_quad(quad):
        shifted = pltpu.roll(ids_cols[...], lax.rem(128 - 4 * quad, 128), 1)
        for q in range(4):
            field = quad * 4 + q
            own_c = shifted[:, q : q + 1] >> 7
            own_r = ids_rows[pl.ds(field, 1), :].astype(jnp.int32) >> 7
            pieces = []
            for block in range(B // 128):
                lanes = own_r[:, block * 128 : (block + 1) * 128]
                total = jnp.zeros((1, 128), F32)
                for other in range(block + 1):
                    same = own_c[other * 128 : (other + 1) * 128] == lanes
                    if other == block:
                        same = same & (iota((128, 128), 0) < iota((128, 128), 1))
                    total = total + jnp.sum(jnp.where(same, 1.0, 0.0), axis=0, keepdims=True)
                pieces.append(total)
            rank = jnp.concatenate(pieces, axis=1).astype(jnp.int32)
            group = ((own_r >> 6) << 3) | (own_r & 7)
            slot = group * GS + ((own_r >> 3) & 7) * CAP + rank
            slot_rows[pl.ds(field, 1), :] = slot.astype(F32)

    def place(chunk):
        @pl.loop(0, FC)
        def _(k):
            field = chunk * FC + k
            row = slot_rows[pl.ds(field, 1), :].astype(jnp.int32)
            data = grads[field]
            half = SLOTS // 2
            for h in range(2):
                hit = iota((half, B), 0) + h * half == row
                placed = jnp.dot(jnp.where(hit, 1.0, 0.0).astype(BF), data, preferred_element_type=F32)
                send[chunk, pl.ds(h * NG // 2, NG // 2), pl.ds(pl.multiple_of(k * GS, GS), GS), :] = (
                    placed.astype(BF).reshape(NG // 2, GS, E)
                )

        pltpu.make_async_copy(send.at[chunk, me], recv.at[chunk, me], recv_sem.at[chunk]).start()

        @pl.loop(1, NG)
        def _(i):
            g = lax.rem(me + i, NG)
            pltpu.make_async_remote_copy(
                src_ref=send.at[chunk, g], dst_ref=recv.at[chunk, me],
                send_sem=send_sem, recv_sem=recv_sem.at[chunk], device_id=device_of(g, z), device_id_type=MESH,
            ).start()

    pl.semaphore_wait(barrier, NG + 1)

    @pl.loop(0, AHEAD * FC // 4)
    def _(quad):
        rank_quad(quad)

        @pl.loop(0, 4 // FC)
        def _(i):
            place(quad * (4 // FC) + i)

    @pl.loop(AHEAD * FC // 4, QUADS)
    def _(quad):
        rank_quad(quad)

    slot_cols[...] = slot_rows[...].T.astype(jnp.int32)

    @pl.loop(0, QUADS)
    def _(quad):
        back = lax.rem(128 - 4 * quad, 128)
        ids = pltpu.roll(ids_cols[...], back, 1)
        slots = pltpu.roll(slot_cols[...], back, 1)
        total = jnp.zeros((NG, 128), F32)
        for q in range(4):
            tag = ((ids[:, q : q + 1] & (RQ - 1)) + 1).astype(F32)
            place = (slots[:, q : q + 1] & (GS - 1)) + q * GS
            right = jnp.where(iota((B, 128), 1) == place, tag, 0.0).astype(BF)
            row = slot_rows[pl.ds(quad * 4 + q, 1), :].astype(jnp.int32)
            group = jnp.where(iota((NG, B), 0) == (row >> 5), 1.0, 0.0).astype(BF)
            total = total + jnp.dot(group, right, preferred_element_type=F32)
        tag_send[pl.ds(quad, NG, stride=8), :] = total

    tag_send[pl.ds(QUADS, NG, stride=8), :] = jnp.zeros((NG, 128), F32)
    def rows8(g):
        return pl.ds(pl.multiple_of(g * 8, 8), 8)

    @pl.loop(1, NG)
    def _(i):
        g = lax.rem(me + i, NG)
        pltpu.make_async_remote_copy(
            src_ref=tag_send.at[rows8(g)], dst_ref=tag_recv.at[rows8(me)],
            send_sem=tag_send_sem, recv_sem=tag_recv_sem, device_id=device_of(g, z), device_id_type=MESH,
        ).start()

    pltpu.make_async_copy(tag_send.at[rows8(me)], tag_recv.at[rows8(me)], tag_recv_sem).start()
    pltpu.make_async_copy(tag_recv, tag_recv, tag_recv_sem).wait()
    tags = tag_recv[...].astype(BF)
    for q in range(4):
        col = iota((128, SLOTS), 1)
        spread = jnp.where(iota((128, SLOTS), 0) == q * GS + (col >> 9) * 16 + (col & 15), 1.0, 0.0).astype(BF)
        wide = jnp.dot(tags, spread, preferred_element_type=F32).reshape(NG, 8, SLOTS)
        source = (iota((NG, 8, SLOTS), 2) & 511) >> 4
        tag = jnp.sum(jnp.where(iota((NG, 8, SLOTS), 0) == source, wide, 0.0), axis=0).astype(jnp.int32)
        row = ((iota((8, SLOTS), 1) & 15) >> 2) * RQ + tag - 1
        wanted[q] = jnp.where(tag > 0, row, -1)

    def tally(chunk):
        pltpu.make_async_copy(recv.at[chunk], recv.at[chunk], recv_sem.at[chunk]).wait()

        @pl.loop(0, FC)
        def _(k):
            field = chunk * FC + k
            want = wanted[field % 4, pl.ds(field // 4, 1), :]
            for h in range(2):
                data = recv[chunk, :, pl.ds(pl.multiple_of(k * GS + h * 16, 16), 16), :].reshape(NG * 16, E)
                hit = iota((4 * RQ, NG * 16), 0) == want[:, h * 512 : (h + 1) * 512]
                rows = jnp.dot(jnp.where(hit, 1.0, 0.0).astype(BF), data, preferred_element_type=F32)
                rows_f32[pl.ds(h * 4 * RQ, 4 * RQ), :] = rows
                part[chunk, pl.ds(h * 4, 4), pl.ds(pl.multiple_of(k * RQ, RQ), RQ), :] = rows.astype(BF).reshape(4, RQ, E)
            out_ref[field] = rows_f32[pl.ds(pl.multiple_of(z * RQ, RQ), RQ), :]

    def owner(d, step):
        away = 4 - step
        return lax.rem(z + (away if d == 0 else NZ - away), NZ)

    def arrived(d, step, chunk):
        size = FC * RQ if step else RQ
        ref = ring.at[d, step, chunk, pl.ds(0, size)]
        pltpu.make_async_copy(ref, ref, ring_recv_sem.at[d, step, chunk]).wait()

    def add(step, chunk):
        for d in range(2):
            arrived(d, step - 1, chunk)
            o = owner(d, step)
            if step == 1:
                part[chunk, o, pl.ds(d * RQ, RQ), :] = (
                    part[chunk, o, pl.ds(d * RQ, RQ), :].astype(F32) + ring[d, 0, chunk, pl.ds(0, RQ), :].astype(F32)
                ).astype(BF)
            else:
                part[chunk, o] = (part[chunk, o].astype(F32) + ring[d, step - 1, chunk].astype(F32)).astype(BF)

    def forward(step, chunk):
        for d in range(2):
            o = owner(d, step)
            src = part.at[chunk, o, pl.ds(d * RQ, RQ)] if step == 0 else part.at[chunk, o]
            dst = ring.at[d, 0, chunk, pl.ds(0, RQ)] if step == 0 else ring.at[d, step, chunk]
            pltpu.make_async_remote_copy(
                src_ref=src, dst_ref=dst, send_sem=ring_send_sem.at[d], recv_sem=ring_recv_sem.at[d, step, chunk],
                device_id=up if d == 0 else down, device_id_type=MESH,
            ).start()

    def finish(chunk):
        for d in range(2):
            arrived(d, 3, chunk)
        both = ring[0, 3, chunk].astype(F32) + ring[1, 3, chunk].astype(F32)
        for k in range(FC):
            out_ref[chunk * FC + k] += both[k * RQ : (k + 1) * RQ]

    @pl.loop(0, C + 4)
    def _(t):
        @pl.when(t + AHEAD < C)
        def _():
            place(t + AHEAD)

        @pl.when(t < C)
        def _():
            tally(t)
            forward(0, t)

        def ring_step(act, step):
            @pl.when((t >= step) & (t < C + step))
            def _():
                act(step, t - step)

        ring_step(add, 1)
        ring_step(add, 2)
        ring_step(forward, 1)
        ring_step(add, 3)
        ring_step(forward, 2)
        ring_step(forward, 3)

        @pl.when(t >= 4)
        def _():
            finish(t - 4)

    sent = send.at[:, pl.ds(0, NG - 1)]
    pltpu.make_async_copy(sent, sent, send_sem).wait()
    tags_sent = tag_send.at[pl.ds(0, (NG - 1) * 8)]
    pltpu.make_async_copy(tags_sent, tags_sent, tag_send_sem).wait()
    for d in range(2):
        for step in range(4):
            ref = ring.at[d, step, :, pl.ds(0, FC * RQ if step else RQ)]
            pltpu.make_async_copy(ref, ref, ring_send_sem.at[d]).wait()


def interact(ids_t, features, pair_grad, table):
    vmem = pl.BlockSpec(memory_space=pltpu.VMEM)
    dma = pltpu.SemaphoreType.DMA
    return pl.pallas_call(
        exchange_kernel,
        out_shape=(jax.ShapeDtypeStruct((F, RQ, E), F32), jax.ShapeDtypeStruct((B, E), F32)),
        in_specs=[vmem, pl.BlockSpec(memory_space=pl.ANY), vmem, vmem],
        out_specs=(vmem, vmem),
        scratch_shapes=[
            pltpu.VMEM((V, B, E), BF),
            pltpu.VMEM((384, B), F32),
            pltpu.VMEM((QUADS, B, 128), BF),
            pltpu.VMEM((4, 128, 32 * SB), BF),
            pltpu.VMEM((NB, 4 * QUADS * SB, 32 * SB), BF),
            pltpu.VMEM((F, B, E), BF),
            pltpu.VMEM((128, B), F32),
            pltpu.VMEM((B, 128), jnp.int32),
            pltpu.VMEM((128, B), F32),
            pltpu.VMEM((B, 128), jnp.int32),
            pltpu.VMEM((NG * 8, 128), F32),
            pltpu.VMEM((NG * 8, 128), F32),
            pltpu.VMEM((4, 8, SLOTS), jnp.int32),
            pltpu.VMEM((C, NG, FC * GS, E), BF),
            pltpu.VMEM((C, NG, FC * GS, E), BF),
            pltpu.VMEM((C, NZ, FC * RQ, E), BF),
            pltpu.VMEM((NZ * RQ, E), F32),
            pltpu.VMEM((2, 4, C, FC * RQ, E), BF),
            dma, dma, dma((C,)), dma, dma, dma((2,)), dma((2, 4, C)),
        ],
        compiler_params=pltpu.CompilerParams(
            collective_id=0, has_side_effects=True, vmem_limit_bytes=63 * 2**20
        ),
        name="interact",
    )(ids_t, features, pair_grad, table)


def local(sample_ids, features, pair_grad):
    table = jnp.asarray(pair_table()).astype(BF)
    return interact(sample_ids.T, features.transpose(1, 0, 2), pair_grad, table)


def solution(mesh):
    placed = (P(("tab", "rep"), None), P(("tab", "rep"), None, None), P(None, ("tab", "rep")))
    return jax.shard_map(
        local,
        mesh=mesh,
        in_specs=placed,
        out_specs=(P(None, ("tab", "rep"), None), P(("tab", "rep"), None)),
        check_vma=False,
    )
```

```python
import functools

import jax
import jax.numpy as jnp
import numpy as np
from jax import lax
from jax.experimental import pallas as pl
from jax.experimental.pallas import tpu as pltpu
from jax.sharding import PartitionSpec as P

RQ = 128
CAP = 4
B = 512
F = 26
E = 128
NZ = 8
NG = 32
GS = NZ * CAP
SLOTS = NG * GS
FC = 2
C = F // FC
AHEAD = 4
QUADS = 7
MESH = pl.DeviceIdType.MESH
BF = jnp.bfloat16
F32 = jnp.float32


V = F + 1
PAIRS = V * F // 2
SB = 8
NB = B // SB


def pair_table():
    row_of, col_of = np.tril_indices(V, -1)
    spread = np.zeros((384, QUADS * 128), np.float32)
    places = np.arange(PAIRS)
    spread[places, row_of * 32 + col_of] = 1.0
    spread[places, col_of * 32 + row_of] = 1.0
    return spread


def device_of(group, z):
    x, core, y = group // 8, (group // 4) % 2, group % 4
    return ((x * NZ + z) * 2 + core, y)


def iota(shape, dim):
    return lax.broadcasted_iota(jnp.int32, shape, dim)


def exchange_kernel(
    ids_ref, feats_hbm, pairs_ref, table_ref, out_ref, dense_ref,
    feats, pairs, picked, expand, left, grads, ids_rows, ids_cols, slot_rows, slot_cols, tag_send, tag_recv, wanted, send, recv, part, rows_f32, ring,
    load_sem, send_sem, recv_sem, tag_send_sem, tag_recv_sem, ring_send_sem, ring_recv_sem,
):
    tab = lax.axis_index("tab")
    y = lax.axis_index("rep")
    x, z, core = tab // (NZ * 2), (tab // 2) % NZ, tab % 2
    me = (x * 2 + core) * 4 + y

    barrier = pltpu.get_barrier_semaphore()
    up = device_of(me, lax.rem(z + 1, NZ))
    down = device_of(me, lax.rem(z + NZ - 1, NZ))

    @pl.loop(1, NG)
    def _(i):
        pl.semaphore_signal(barrier, inc=1, device_id=device_of(lax.rem(me + i, NG), z), device_id_type=MESH)

    pl.semaphore_signal(barrier, inc=1, device_id=up, device_id_type=MESH)
    pl.semaphore_signal(barrier, inc=1, device_id=down, device_id_type=MESH)

    load = pltpu.make_async_copy(feats_hbm, feats, load_sem)
    load.start()

    pairs[...] = jnp.zeros(pairs.shape, F32)
    pairs[pl.ds(0, PAIRS), :] = pairs_ref[...].astype(F32)
    by_sample = pairs[...].T.astype(BF)
    for quad in range(QUADS):
        picked[quad] = jnp.dot(
            by_sample, table_ref[:, quad * 128 : (quad + 1) * 128], preferred_element_type=F32
        ).astype(BF)
    for q in range(4):
        expand[q] = jnp.where(
            iota((128, 32 * SB), 0) == q * 32 + (iota((128, 32 * SB), 1) >> 3), 1.0, 0.0
        ).astype(BF)

    @pl.loop(0, QUADS)
    def _(quad):
        own = iota((1, SB, 32 * SB), 1) == (iota((1, SB, 32 * SB), 2) & (SB - 1))
        for pair in range(2):
            both = [
                jnp.dot(picked[quad], expand[pair * 2 + q], preferred_element_type=F32).reshape(NB, SB, 32 * SB)
                for q in range(2)
            ]
            both = jnp.concatenate([jnp.where(own, wide, 0.0) for wide in both], axis=1)
            left[:, pl.ds(pl.multiple_of((quad * 2 + pair) * 2 * SB, 2 * SB), 2 * SB), :] = both.astype(BF)

    load.wait()

    @pl.loop(0, NB // 2, unroll=4)
    def _(g):
        at = pl.ds(pl.multiple_of(g * 2 * SB, 2 * SB), 2 * SB)
        wide = feats[:, at, :].astype(F32)
        results = []
        for h in range(2):
            right = jnp.concatenate([wide[:, h * SB : (h + 1) * SB], jnp.zeros((32 - V, SB, E), F32)], axis=0)
            right = right.reshape(32 * SB, E).astype(BF)
            result = jnp.dot(left[g * 2 + h], right, preferred_element_type=F32)
            results.append(result.reshape(4 * QUADS, SB, E))
        result = jnp.concatenate(results, axis=1)
        dense_ref[at, :] = result[0]
        grads[:, at, :] = result[1:V].astype(BF)

    ids_rows[...] = jnp.zeros(ids_rows.shape, F32)
    ids_rows[pl.ds(0, F), :] = ids_ref[...].astype(F32)
    ids_cols[...] = ids_rows[...].T.astype(jnp.int32)

    slot_rows[...] = jnp.zeros(slot_rows.shape, F32)

    def rank_quad(quad):
        shifted = pltpu.roll(ids_cols[...], lax.rem(128 - 4 * quad, 128), 1)
        for q in range(4):
            field = quad * 4 + q
            own_c = shifted[:, q : q + 1] >> 7
            own_r = ids_rows[pl.ds(field, 1), :].astype(jnp.int32) >> 7
            pieces = []
            for block in range(B // 128):
                lanes = own_r[:, block * 128 : (block + 1) * 128]
                total = jnp.zeros((1, 128), F32)
                for other in range(block + 1):
                    same = own_c[other * 128 : (other + 1) * 128] == lanes
                    if other == block:
                        same = same & (iota((128, 128), 0) < iota((128, 128), 1))
                    total = total + jnp.sum(jnp.where(same, 1.0, 0.0), axis=0, keepdims=True)
                pieces.append(total)
            rank = jnp.concatenate(pieces, axis=1).astype(jnp.int32)
            group = ((own_r >> 6) << 3) | (own_r & 7)
            slot = group * GS + ((own_r >> 3) & 7) * CAP + rank
            slot_rows[pl.ds(field, 1), :] = slot.astype(F32)

    def place(chunk):
        @pl.loop(0, FC, unroll=2)
        def _(k):
            field = chunk * FC + k
            row = slot_rows[pl.ds(field, 1), :].astype(jnp.int32)
            data = grads[field]
            half = SLOTS // 2
            for h in range(2):
                hit = iota((half, B), 0) + h * half == row
                placed = jnp.dot(jnp.where(hit, 1.0, 0.0).astype(BF), data, preferred_element_type=F32)
                send[chunk, pl.ds(h * NG // 2, NG // 2), pl.ds(pl.multiple_of(k * GS, GS), GS), :] = (
                    placed.astype(BF).reshape(NG // 2, GS, E)
                )

        pltpu.make_async_copy(send.at[chunk, me], recv.at[chunk, me], recv_sem.at[chunk]).start()

        @pl.loop(1, NG)
        def _(i):
            g = lax.rem(me + i, NG)
            pltpu.make_async_remote_copy(
                src_ref=send.at[chunk, g], dst_ref=recv.at[chunk, me],
                send_sem=send_sem, recv_sem=recv_sem.at[chunk], device_id=device_of(g, z), device_id_type=MESH,
            ).start()

    pl.semaphore_wait(barrier, NG + 1)

    @pl.loop(0, AHEAD * FC // 4)
    def _(quad):
        rank_quad(quad)

        @pl.loop(0, 4 // FC)
        def _(i):
            place(quad * (4 // FC) + i)

    @pl.loop(AHEAD * FC // 4, QUADS)
    def _(quad):
        rank_quad(quad)

    slot_cols[...] = slot_rows[...].T.astype(jnp.int32)

    @pl.loop(0, QUADS)
    def _(quad):
        back = lax.rem(128 - 4 * quad, 128)
        ids = pltpu.roll(ids_cols[...], back, 1)
        slots = pltpu.roll(slot_cols[...], back, 1)
        total = jnp.zeros((NG, 128), F32)
        for q in range(4):
            tag = ((ids[:, q : q + 1] & (RQ - 1)) + 1).astype(F32)
            place = (slots[:, q : q + 1] & (GS - 1)) + q * GS
            right = jnp.where(iota((B, 128), 1) == place, tag, 0.0).astype(BF)
            row = slot_rows[pl.ds(quad * 4 + q, 1), :].astype(jnp.int32)
            group = jnp.where(iota((NG, B), 0) == (row >> 5), 1.0, 0.0).astype(BF)
            total = total + jnp.dot(group, right, preferred_element_type=F32)
        tag_send[pl.ds(quad, NG, stride=8), :] = total

    tag_send[pl.ds(QUADS, NG, stride=8), :] = jnp.zeros((NG, 128), F32)
    def rows8(g):
        return pl.ds(pl.multiple_of(g * 8, 8), 8)

    @pl.loop(1, NG)
    def _(i):
        g = lax.rem(me + i, NG)
        pltpu.make_async_remote_copy(
            src_ref=tag_send.at[rows8(g)], dst_ref=tag_recv.at[rows8(me)],
            send_sem=tag_send_sem, recv_sem=tag_recv_sem, device_id=device_of(g, z), device_id_type=MESH,
        ).start()

    pltpu.make_async_copy(tag_send.at[rows8(me)], tag_recv.at[rows8(me)], tag_recv_sem).start()
    pltpu.make_async_copy(tag_recv, tag_recv, tag_recv_sem).wait()
    tags = tag_recv[...].astype(BF)
    for q in range(4):
        col = iota((128, SLOTS), 1)
        spread = jnp.where(iota((128, SLOTS), 0) == q * GS + (col >> 9) * 16 + (col & 15), 1.0, 0.0).astype(BF)
        wide = jnp.dot(tags, spread, preferred_element_type=F32).reshape(NG, 8, SLOTS)
        source = (iota((NG, 8, SLOTS), 2) & 511) >> 4
        tag = jnp.sum(jnp.where(iota((NG, 8, SLOTS), 0) == source, wide, 0.0), axis=0).astype(jnp.int32)
        row = ((iota((8, SLOTS), 1) & 15) >> 2) * RQ + tag - 1
        wanted[q] = jnp.where(tag > 0, row, -1)

    def tally(chunk):
        pltpu.make_async_copy(recv.at[chunk], recv.at[chunk], recv_sem.at[chunk]).wait()

        @pl.loop(0, FC, unroll=2)
        def _(k):
            field = chunk * FC + k
            want = wanted[field % 4, pl.ds(field // 4, 1), :]
            for h in range(2):
                data = recv[chunk, :, pl.ds(pl.multiple_of(k * GS + h * 16, 16), 16), :].reshape(NG * 16, E)
                hit = iota((4 * RQ, NG * 16), 0) == want[:, h * 512 : (h + 1) * 512]
                rows = jnp.dot(jnp.where(hit, 1.0, 0.0).astype(BF), data, preferred_element_type=F32)
                rows_f32[pl.ds(h * 4 * RQ, 4 * RQ), :] = rows
                part[chunk, pl.ds(h * 4, 4), pl.ds(pl.multiple_of(k * RQ, RQ), RQ), :] = rows.astype(BF).reshape(4, RQ, E)
            out_ref[field] = rows_f32[pl.ds(pl.multiple_of(z * RQ, RQ), RQ), :]

    def owner(d, step):
        away = 4 - step
        return lax.rem(z + (away if d == 0 else NZ - away), NZ)

    def arrived(d, step, chunk):
        size = FC * RQ if step else RQ
        ref = ring.at[d, step, chunk, pl.ds(0, size)]
        pltpu.make_async_copy(ref, ref, ring_recv_sem.at[d, step, chunk]).wait()

    def add(step, chunk):
        for d in range(2):
            arrived(d, step - 1, chunk)
            o = owner(d, step)
            if step == 1:
                part[chunk, o, pl.ds(d * RQ, RQ), :] = (
                    part[chunk, o, pl.ds(d * RQ, RQ), :].astype(F32) + ring[d, 0, chunk, pl.ds(0, RQ), :].astype(F32)
                ).astype(BF)
            else:
                part[chunk, o] = (part[chunk, o].astype(F32) + ring[d, step - 1, chunk].astype(F32)).astype(BF)

    def forward(step, chunk):
        for d in range(2):
            o = owner(d, step)
            src = part.at[chunk, o, pl.ds(d * RQ, RQ)] if step == 0 else part.at[chunk, o]
            dst = ring.at[d, 0, chunk, pl.ds(0, RQ)] if step == 0 else ring.at[d, step, chunk]
            pltpu.make_async_remote_copy(
                src_ref=src, dst_ref=dst, send_sem=ring_send_sem.at[d], recv_sem=ring_recv_sem.at[d, step, chunk],
                device_id=up if d == 0 else down, device_id_type=MESH,
            ).start()

    def finish(chunk):
        for d in range(2):
            arrived(d, 3, chunk)
        both = ring[0, 3, chunk].astype(F32) + ring[1, 3, chunk].astype(F32)
        for k in range(FC):
            out_ref[chunk * FC + k] += both[k * RQ : (k + 1) * RQ]

    @pl.loop(0, C + 4)
    def _(t):
        @pl.when(t + AHEAD < C)
        def _():
            place(t + AHEAD)

        @pl.when(t < C)
        def _():
            tally(t)
            forward(0, t)

        def ring_step(act, step):
            @pl.when((t >= step) & (t < C + step))
            def _():
                act(step, t - step)

        ring_step(add, 1)
        ring_step(add, 2)
        ring_step(forward, 1)
        ring_step(add, 3)
        ring_step(forward, 2)
        ring_step(forward, 3)

        @pl.when(t >= 4)
        def _():
            finish(t - 4)

    sent = send.at[:, pl.ds(0, NG - 1)]
    pltpu.make_async_copy(sent, sent, send_sem).wait()
    tags_sent = tag_send.at[pl.ds(0, (NG - 1) * 8)]
    pltpu.make_async_copy(tags_sent, tags_sent, tag_send_sem).wait()
    for d in range(2):
        for step in range(4):
            ref = ring.at[d, step, :, pl.ds(0, FC * RQ if step else RQ)]
            pltpu.make_async_copy(ref, ref, ring_send_sem.at[d]).wait()


def interact(ids_t, features, pair_grad, table):
    vmem = pl.BlockSpec(memory_space=pltpu.VMEM)
    dma = pltpu.SemaphoreType.DMA
    return pl.pallas_call(
        exchange_kernel,
        out_shape=(jax.ShapeDtypeStruct((F, RQ, E), F32), jax.ShapeDtypeStruct((B, E), F32)),
        in_specs=[vmem, pl.BlockSpec(memory_space=pl.ANY), vmem, vmem],
        out_specs=(vmem, vmem),
        scratch_shapes=[
            pltpu.VMEM((V, B, E), BF),
            pltpu.VMEM((384, B), F32),
            pltpu.VMEM((QUADS, B, 128), BF),
            pltpu.VMEM((4, 128, 32 * SB), BF),
            pltpu.VMEM((NB, 4 * QUADS * SB, 32 * SB), BF),
            pltpu.VMEM((F, B, E), BF),
            pltpu.VMEM((128, B), F32),
            pltpu.VMEM((B, 128), jnp.int32),
            pltpu.VMEM((128, B), F32),
            pltpu.VMEM((B, 128), jnp.int32),
            pltpu.VMEM((NG * 8, 128), F32),
            pltpu.VMEM((NG * 8, 128), F32),
            pltpu.VMEM((4, 8, SLOTS), jnp.int32),
            pltpu.VMEM((C, NG, FC * GS, E), BF),
            pltpu.VMEM((C, NG, FC * GS, E), BF),
            pltpu.VMEM((C, NZ, FC * RQ, E), BF),
            pltpu.VMEM((NZ * RQ, E), F32),
            pltpu.VMEM((2, 4, C, FC * RQ, E), BF),
            dma, dma, dma((C,)), dma, dma, dma((2,)), dma((2, 4, C)),
        ],
        compiler_params=pltpu.CompilerParams(
            collective_id=0, has_side_effects=True, vmem_limit_bytes=63 * 2**20
        ),
        name="interact",
    )(ids_t, features, pair_grad, table)


def local(sample_ids, features, pair_grad):
    table = jnp.asarray(pair_table()).astype(BF)
    return interact(sample_ids.T, features.transpose(1, 0, 2), pair_grad, table)


def solution(mesh):
    placed = (P(("tab", "rep"), None), P(("tab", "rep"), None, None), P(None, ("tab", "rep")))
    return jax.shard_map(
        local,
        mesh=mesh,
        in_specs=placed,
        out_specs=(P(None, ("tab", "rep"), None), P(("tab", "rep"), None)),
        check_vma=False,
    )
```
